32 devices in a mesh: tm: 4 (over y, x), blk: 8 (over z, core).
Axes of the slice: x: 2, y: 2, z: 4, core: 2. Of those that a mesh axis runs over, the one named last changes fastest.
Arguments:
- chi_bar: bfloat16 [4, 8, 3, 128, 128], P('tm', 'blk'), may hold values from -0.023925781 to 0.023925781
- cos_table: int32 [8, 4], replicated, may hold values from -1024 to 1024
- partner: int32 [8, 3], P('blk'), may hold values from 0 to 7, all different within a row
- tensor: bfloat16 [1024, 2, 2048], P('blk'), may hold values from -6 to 6
- dens_tensor: bfloat16 [1024, 2, 2048], P('blk'), may hold values from -6 to 6
- decay: float32 [8, 2, 2048], P('tm'), may hold values from 0.1 to 1
Outputs:
- tensor_grad: bfloat16 [8, 1024, 2, 2048], P('tm', 'blk')
- density_grad: float32 [1024, 128], P('blk')
The draws below stay inside these ranges and needn't reach their ends.
Inputs may be any that keep to these rules, and one draw needn't show every extreme that they name: `partner`: each row names 3 different blocks; every block is named by some row.
All inputs are finite; a program needn't handle non-finite values.
Results may differ from the reference program's by a relative error of at most 0.011.
Values may be sent and summed in bfloat16 or wider, within the bound.
A program may use at most 64 MiB of HBM per device.

```python
import math
import jax
import jax.numpy as jnp
from jax import lax

BLOCK = 128
TILE_COLS = 2048
TILES = 2
NFREQ = 4
NTIME = 8
NPAIR = 3
AUX = 1024
N_BLK = 8


def with_ends(drawn, key, least, largest):
    longest = drawn.shape.index(max(drawn.shape))
    spots = []
    for shift in (0, 1):
        where = [jax.random.randint(jax.random.fold_in(key, axis), (), 0, length) for axis, length in enumerate(drawn.shape)]
        where[longest] = (where[longest] + shift) % drawn.shape[longest]
        spots.append(tuple(where))
    return drawn.at[spots[0]].set(least).at[spots[1]].set(largest)


def steps_of(own_key, extent, cuts, low, high):
    factor_of, own = 1.0, jax.random.fold_in(own_key, 6)
    for dim, shards_of in cuts:
        steps = jnp.exp(jax.random.uniform(jax.random.fold_in(own, dim), (shards_of,), jnp.float32, low / len(cuts), high / len(cuts)))
        factor_of = factor_of * jnp.repeat(steps, extent[dim] // shards_of).reshape([-1 if axis == dim else 1 for axis in range(len(extent))])
    return factor_of


def distinct(stream_key, rows, count, top, lift):
    sequence = jax.random.permutation(jax.random.fold_in(stream_key, 1), count)
    pull = sequence
    for power in range(3):
        pull = pull * pull // count
    pull = pull * lift // count
    tickets = jax.random.randint(jax.random.fold_in(stream_key, 2), (rows, count), 0, 4096) + pull
    sure = jax.random.permutation(jax.random.fold_in(stream_key, 3), rows)[jnp.arange(count) % rows]
    tickets = jnp.where(jnp.arange(rows)[:, None] == sure[None, :], 1 << 14, tickets)
    merit = tickets * count + jnp.arange(count)
    return lax.top_k(merit.astype(jnp.int32), top)[1].astype(jnp.int32)


def gaussian(own_key, extent, scale, most, pieces=(), held_as=jnp.bfloat16):
    array = scale * jax.random.normal(own_key, extent, jnp.float32)
    if pieces:
        array = array * steps_of(own_key, extent, pieces, -0.22, 0.18)
    return jnp.clip(array, -most, most).astype(held_as)


def setup_inputs(seed: int = 0) -> dict:
    seeds = jax.random.split(jax.random.key(seed), 7)
    chi_bar = gaussian(seeds[0], (NFREQ, N_BLK, NPAIR, BLOCK, BLOCK), 0.004, 0.023925781, ((0, 4), (1, 8)))
    cos_table = with_ends(jax.random.randint(seeds[1], (NTIME, NFREQ), -1024, 1025), jax.random.fold_in(seeds[1], 1), -1024, 1024).astype(jnp.int32)
    partner = distinct(seeds[2], N_BLK, N_BLK, NPAIR, 6144)
    tensor = gaussian(seeds[3], (AUX, TILES, TILE_COLS), 1.0, 6.0, ((0, 8),))
    dens_tensor = gaussian(seeds[4], (AUX, TILES, TILE_COLS), 1.0, 6.0, ((0, 8),))
    decay = jnp.clip(jnp.exp(math.log(1.0) - 2.3025851 * jax.random.uniform(seeds[5], (NTIME, TILES, TILE_COLS), jnp.float32) ** steps_of(seeds[5], (NTIME, TILES, TILE_COLS), ((0, 4),), -0.2, 0.2)), 0.1, 1.0)
    return {"chi_bar": chi_bar, "cos_table": cos_table, "partner": partner, "tensor": tensor, "dens_tensor": dens_tensor, "decay": decay}


def reference(chi_bar, cos_table, partner, tensor, dens_tensor, decay):
    hp = lax.Precision.HIGHEST
    weights = cos_table.astype(jnp.float32) / 1024.0
    width = TILES * TILE_COLS
    inv_width = 1.0 / math.sqrt(width)
    chi_full = chi_bar.astype(jnp.float32)
    onehot = (partner[:, :, None] == jnp.arange(N_BLK, dtype=jnp.int32)[None, None, :]).astype(jnp.float32)
    tens = tensor.reshape(N_BLK, BLOCK, width)
    dens = dens_tensor.reshape(N_BLK, BLOCK, width)
    tens_f = tens.astype(jnp.float32)

    def one_time(index):
        gbar = jnp.einsum('w,wqkab->qkab', weights[index], chi_full, precision=hp).astype(jnp.bfloat16)
        factor = decay[index].reshape(1, 1, width)
        scaled = (tens_f * factor).astype(jnp.bfloat16).astype(jnp.float32)
        dscaled = (dens.astype(jnp.float32) * factor).astype(jnp.bfloat16).astype(jnp.float32)
        metric = (jnp.einsum('qaj,qbj->qab', tens_f, dscaled) * inv_width).astype(jnp.bfloat16)
        term = jnp.einsum('qkab,qbc->qkac', gbar.astype(jnp.float32), metric.astype(jnp.float32))
        collected = jnp.einsum('qkp,qkac->pac', onehot, term, precision=hp).astype(jnp.bfloat16).astype(jnp.float32)
        grad = jnp.einsum('pab,pbj->paj', collected, scaled) + jnp.einsum('pba,pbj->paj', collected, dscaled)
        grad = grad.astype(jnp.bfloat16)
        dpart = jnp.einsum('paj,pbj->pab', grad.astype(jnp.float32), dscaled) * inv_width
        return (grad, dpart)
    grads, dparts = lax.map(one_time, jnp.arange(NTIME, dtype=jnp.int32))
    tensor_grad = grads.reshape(NTIME, AUX, TILES, TILE_COLS)
    density_grad = lax.optimization_barrier(jnp.sum(dparts, axis=0)).reshape(AUX, BLOCK)
    return (tensor_grad, density_grad)
```

```python
import functools
import math

import jax
import jax.numpy as jnp
from jax import lax
from jax.experimental import pallas as pl
from jax.experimental.pallas import tpu as pltpu
from jax.sharding import PartitionSpec as P

F32 = jnp.float32
BF16 = jnp.bfloat16
MESH = pl.DeviceIdType.MESH


def dot(a, b, dims=((1,), (0,)), precision=None):
    return lax.dot_general(a, b, (dims, ((), ())), preferred_element_type=F32, precision=precision)


def steps(count, body):
    if count <= 8:
        for i in range(count):
            body(i)
    else:
        lax.fori_loop(0, count, lambda i, c: (body(i), c)[1], 0)


def kernel(
    n_tm, n_blk, parts, chunk,
    cos_ref, partner_ref, chi_ref, tens_ref, dens_ref, decay_ref,
    grad_ref, density_ref,
    partner_vec, chi_all, tens, dens, decay, sd, metric, corr, own_term, out_term, in_term, pair_vec, outgoing, arrived,
    dpart_out, dpart_in,
    load_sem, chi_send, chi_recv, sib_send, sib_recv, vec_send, vec_recv,
    a2a_send, a2a_recv, own_sem, dp_send, dp_recv,
):
    tm = lax.axis_index("tm")
    blk = lax.axis_index("blk")
    chips = n_blk // 2
    chip = blk // 2
    core = blk % 2
    n_pair, block, _ = chi_ref.shape
    times = decay.shape[0]
    half = times // 2
    rows2, width2 = tens.shape
    inv_width = 1.0 / math.sqrt(2 * width2)
    part = block // parts
    hp = lax.Precision.HIGHEST

    loads = [
        pltpu.make_async_copy(dens_ref.reshape(*dens.shape), dens, load_sem.at[0]),
        pltpu.make_async_copy(decay_ref, decay, load_sem.at[1]),
        pltpu.make_async_copy(tens_ref.reshape(*tens.shape), tens, load_sem.at[2]),
        pltpu.make_async_copy(chi_ref, chi_all.at[tm], load_sem.at[3]),
    ]
    for copy in loads:
        copy.start()

    partner_vec[...] = jnp.full(partner_vec.shape, -1, jnp.int32)
    for k in range(n_pair):
        partner_vec[k : k + 1, :] = jnp.full((1, block), partner_ref[0, k], jnp.int32)

    def tm_peer(o):
        return lax.rem(tm + o, n_tm)

    def blk_peer(o):
        return lax.rem(blk + o, n_blk)

    barrier = pltpu.get_barrier_semaphore()
    for o in range(1, n_tm):
        pl.semaphore_signal(barrier, inc=1, device_id={"tm": tm_peer(o)}, device_id_type=MESH)
    steps(n_blk - 1, lambda i: pl.semaphore_signal(
        barrier, inc=1, device_id={"blk": blk_peer(i + 1)}, device_id_type=MESH))
    loads.pop().wait()
    pl.semaphore_wait(barrier, n_tm + n_blk - 2)

    def chi_copy(o, r):
        rows = pl.ds(r * part, part)
        return pltpu.make_async_remote_copy(
            src_ref=chi_all.at[tm, :, rows, :],
            dst_ref=chi_all.at[tm, :, rows, :],
            send_sem=chi_send.at[o - 1, r],
            recv_sem=chi_recv.at[o - 1, r],
            device_id={"tm": tm_peer(o)},
            device_id_type=MESH,
        )

    def chi_arrival(o, r):
        rows = pl.ds(r * part, part)
        source = lax.rem(tm + n_tm - o, n_tm)
        return pltpu.make_async_remote_copy(
            src_ref=chi_all.at[tm, :, rows, :],
            dst_ref=chi_all.at[source, :, rows, :],
            send_sem=chi_send.at[o - 1, r],
            recv_sem=chi_recv.at[o - 1, r],
            device_id={"tm": tm_peer(o)},
            device_id_type=MESH,
        )

    sibling = {"blk": chip * 2 + 1 - core}
    vec_copy = pltpu.make_async_remote_copy(
        src_ref=partner_vec, dst_ref=pair_vec, send_sem=vec_send, recv_sem=vec_recv,
        device_id=sibling, device_id_type=MESH)
    vec_copy.start()
    for r in range(parts):
        for o in range(1, n_tm):
            chi_copy(o, r).start()

    for copy in loads:
        copy.wait()
    even = lax.broadcasted_iota(jnp.int32, (rows2, chunk), 0) % 2 == 0
    same = (lax.broadcasted_iota(jnp.int32, (rows2, rows2), 0) % 2) == (
        lax.broadcasted_iota(jnp.int32, (rows2, rows2), 1) % 2)
    spread = (
        lax.broadcasted_iota(jnp.int32, (rows2, block), 0) // 2
        == lax.broadcasted_iota(jnp.int32, (rows2, block), 1)
    ).astype(F32)

    def fold(m):
        m = jnp.where(same, m, 0.0)
        return dot(dot(spread, m, ((0,), (0,)), hp), spread, precision=hp)

    for t in range(times):
        m2 = jnp.zeros((rows2, rows2), F32)
        for j in range(width2 // chunk):
            cols = slice(j * chunk, (j + 1) * chunk)
            factor = jnp.where(even, decay[t, 0:1, cols], decay[t, 1:2, cols])
            x = tens[:, cols]
            d = (dens[:, cols].astype(F32) * factor).astype(BF16)
            sd[t, :rows2, cols] = (x.astype(F32) * factor).astype(BF16)
            sd[t, rows2:, cols] = d
            m2 = m2 + dot(x, d, ((1,), (1,)))
        metric[t] = (fold(m2) * inv_width).astype(BF16)

    def sib_copy(r):
        return pltpu.make_async_remote_copy(
            src_ref=out_term.at[r], dst_ref=in_term.at[r],
            send_sem=sib_send.at[r], recv_sem=sib_recv.at[r],
            device_id=sibling, device_id_type=MESH)

    def a2a_copy(o, c, r):
        dest = lax.rem(chip + o, chips) * 2 + c
        return pltpu.make_async_remote_copy(
            src_ref=outgoing.at[r, dest],
            dst_ref=arrived.at[chip, core, :, pl.ds(r * part, part), :],
            send_sem=a2a_send.at[o, c, r],
            recv_sem=a2a_recv.at[o, core, r],
            device_id={"blk": dest}, device_id_type=MESH)

    def a2a_arrival(o, c, r):
        source = lax.rem(chip + chips - o, chips)
        return pltpu.make_async_remote_copy(
            src_ref=outgoing.at[r, 0],
            dst_ref=arrived.at[source, c, :, pl.ds(r * part, part), :],
            send_sem=a2a_send.at[o, c, r],
            recv_sem=a2a_recv.at[o, c, r],
            device_id={"blk": blk}, device_id_type=MESH)

    def own_copy(r):
        return pltpu.make_async_copy(
            outgoing.at[r, blk],
            arrived.at[chip, core, :, pl.ds(r * part, part), :],
            own_sem.at[r])

    for r in range(parts):
        rows = pl.ds(r * part, part)
        for o in range(1, n_tm):
            chi_arrival(o, r).wait_recv()
        for t in range(times):
            owner = (1 - core if t < half else core)
            slot = t % half
            time = owner * half + slot
            weights = [cos_ref[w, tm * times + time].astype(F32) / 1024.0 for w in range(n_tm)]
            m = metric[time]

            def one(k):
                g = weights[0] * chi_all[0, k, rows, :].astype(F32)
                for w in range(1, n_tm):
                    g = g + weights[w] * chi_all[w, k, rows, :].astype(F32)
                term = dot(g.astype(BF16), m)
                if t < half:
                    out_term[r, k, slot] = term.astype(BF16)
                else:
                    own_term[r, k, slot] = term

            steps(n_pair, one)
            if t == half - 1:
                sib_copy(r).start()
        if r == 0:
            vec_copy.wait_recv()
        sib_copy(r).wait_recv()

        def bin_of(dest):
            for slot in range(half):
                total = jnp.zeros((part, block), F32)

                def add(k, total):
                    mine = jnp.full((1, block), partner_ref[0, k], jnp.int32) == dest
                    theirs = pair_vec[pl.ds(k, 1), :] == dest
                    total = total + jnp.where(mine, own_term[r, k, slot], 0.0)
                    return total + jnp.where(theirs, in_term[r, k, slot].astype(F32), 0.0)

                if n_pair <= 8:
                    for k in range(n_pair):
                        total = add(k, total)
                else:
                    total = lax.fori_loop(0, n_pair, add, total)
                outgoing[r, dest, slot] = total.astype(BF16)

        def send(i):
            o = chips - 1 - i
            for c in range(2):
                dest = lax.rem(chip + o, chips) * 2 + c
                bin_of(dest)
                a2a_copy(o, c, r).start()

        steps(chips - 1, send)
        bin_of(blk)
        own_copy(r).start()
        bin_of(chip * 2 + 1 - core)
        pltpu.make_async_remote_copy(
            src_ref=outgoing.at[r, chip * 2 + 1 - core],
            dst_ref=arrived.at[chip, core, :, pl.ds(r * part, part), :],
            send_sem=a2a_send.at[0, 0, r],
            recv_sem=a2a_recv.at[0, 0, r],
            device_id=sibling, device_id_type=MESH).start()

    def sib_arrival(r):
        return pltpu.make_async_remote_copy(
            src_ref=outgoing.at[r, 0],
            dst_ref=arrived.at[chip, 1 - core, :, pl.ds(r * part, part), :],
            send_sem=a2a_send.at[0, 0, r],
            recv_sem=a2a_recv.at[0, 0, r],
            device_id=sibling, device_id_type=MESH)

    for t in range(times):
        for side in range(2):
            m2 = jnp.zeros((rows2, rows2), F32)
            for j in range(width2 // chunk):
                cols = slice(j * chunk, (j + 1) * chunk)
                m2 = m2 + dot(
                    sd[t, side * rows2 : (side + 1) * rows2, cols], sd[t, rows2:, cols], ((1,), (1,)))
            corr[t, side * block : (side + 1) * block, :] = fold(m2) * inv_width

    for r in range(parts):
        own_copy(r).wait()
        sib_arrival(r).wait_recv()

        def wait_for(i):
            for c in range(2):
                a2a_arrival(i + 1, c, r).wait_recv()

        steps(chips - 1, wait_for)

    spread_b = spread.astype(BF16)
    dpart = jnp.zeros((block, block), F32)
    sums = []
    for t in range(times):
        def more(i, total):
            return total + arrived[i, t // half, t % half].astype(F32)

        total = jnp.zeros((block, block), F32)
        if chips <= 8:
            for i in range(chips):
                total = more(i, total)
        else:
            total = lax.fori_loop(0, chips, more, total)
        total = total.astype(BF16)
        turned = total.astype(F32).T.astype(BF16)
        sums.append((total, turned))
        both = jnp.concatenate([total, turned], axis=1)
        rest = corr[t]
        for _ in range(3):
            piece = rest.astype(BF16)
            rest = rest - piece.astype(F32)
            dpart = dpart + dot(both, piece)
    dpart_out[...] = dpart.astype(BF16)

    def dp_copy(o, source):
        return pltpu.make_async_remote_copy(
            src_ref=dpart_out, dst_ref=dpart_in.at[source],
            send_sem=dp_send.at[o - 1], recv_sem=dp_recv.at[o - 1],
            device_id={"tm": tm_peer(o)}, device_id_type=MESH)

    for o in range(1, n_tm):
        dp_copy(o, tm).start()
    dpart_in[tm] = dpart_out[...]

    for t in range(times):
        wide = [
            jnp.where(same, dot(dot(spread_b, c).astype(BF16), spread_b, ((1,), (1,))), 0.0).astype(BF16)
            for c in sums[t]
        ]
        both = jnp.concatenate(wide, axis=1)
        for j in range(width2 // chunk):
            cols = slice(j * chunk, (j + 1) * chunk)
            grad_ref[t, :, cols] = dot(both, sd[t, :, cols]).astype(BF16)
    for o in range(1, n_tm):
        dp_copy(o, lax.rem(tm + n_tm - o, n_tm)).wait_recv()
    density = dpart_in[0].astype(F32)
    for w in range(1, n_tm):
        density = density + dpart_in[w].astype(F32)
    density_ref[...] = density
    vec_copy.wait_send()
    for r in range(parts):
        for o in range(1, n_tm):
            chi_copy(o, r).wait_send()
        sib_copy(r).wait_send()
        sib_arrival(r).wait_send()

        def sent(i):
            for c in range(2):
                a2a_copy(i + 1, c, r).wait_send()

        steps(chips - 1, sent)
    for o in range(1, n_tm):
        dp_copy(o, tm).wait_send()


def deliver(grad_ref, density_ref, grad_out, density_out, sem):
    copies = [
        pltpu.make_async_copy(grad_ref.at[t], grad_out.at[t].reshape(*grad_ref.shape[1:]), sem.at[t])
        for t in range(grad_ref.shape[0])
    ]
    copies.append(pltpu.make_async_copy(density_ref, density_out, sem.at[len(copies)]))
    for copy in copies:
        copy.start()
    for copy in copies:
        copy.wait()


def on_device(n_tm, n_blk, chi_bar, cos_table, partner, tensor, dens_tensor, decay):
    n_pair, block = chi_bar.shape[2], chi_bar.shape[3]
    times = decay.shape[0]
    half = times // 2
    rows2, width2 = block * tensor.shape[1], tensor.shape[2]
    chips = n_blk // 2
    parts = 2
    chunk = 512
    part = block // parts
    any_ = pl.BlockSpec(memory_space=pl.ANY)
    smem = pl.BlockSpec(memory_space=pltpu.SMEM)
    vmem = pl.BlockSpec(memory_space=pltpu.VMEM)
    pad = -n_pair % 8
    dma = pltpu.SemaphoreType.DMA
    grad, density = pl.pallas_call(
        functools.partial(kernel, n_tm, n_blk, parts, chunk),
        out_shape=(
            pltpu.VMEM((times, rows2, width2), BF16),
            pltpu.VMEM((block, block), F32),
        ),
        in_specs=[smem, smem, any_, any_, any_, any_],
        out_specs=(vmem, vmem),
        scratch_shapes=[
            pltpu.VMEM((n_pair + pad, block), jnp.int32),
            pltpu.VMEM((n_tm, n_pair, block, block), BF16),
            pltpu.VMEM((rows2, width2), BF16),
            pltpu.VMEM((rows2, width2), BF16),
            pltpu.VMEM(decay.shape, F32),
            pltpu.VMEM((times, 2 * rows2, width2), BF16),
            pltpu.VMEM((times, block, block), BF16),
            pltpu.VMEM((times, 2 * block, block), F32),
            pltpu.VMEM((parts, n_pair, half, part, block), F32),
            pltpu.VMEM((parts, n_pair, half, part, block), BF16),
            pltpu.VMEM((parts, n_pair, half, part, block), BF16),
            pltpu.VMEM((n_pair + pad, block), jnp.int32),
            pltpu.VMEM((parts, n_blk, half, part, block), BF16),
            pltpu.VMEM((chips, 2, half, block, block), BF16),
            pltpu.VMEM((block, block), BF16),
            pltpu.VMEM((n_tm, block, block), BF16),
            dma((4,)),
            dma((n_tm - 1, parts)), dma((n_tm - 1, parts)),
            dma((parts,)), dma((parts,)),
            dma, dma,
            dma((chips, 2, parts)), dma((chips, 2, parts)),
            dma((parts,)),
            dma((n_tm - 1,)), dma((n_tm - 1,)),
        ],
        compiler_params=pltpu.CompilerParams(collective_id=0, has_side_effects=True),
    )(
        cos_table.T, partner,
        chi_bar.reshape(n_pair, block, block),
        tensor, dens_tensor, decay,
    )
    return pl.pallas_call(
        deliver,
        out_shape=(
            jax.ShapeDtypeStruct((times, *tensor.shape), BF16),
            jax.ShapeDtypeStruct((block, block), F32),
        ),
        in_specs=[vmem, vmem],
        out_specs=(any_, any_),
        scratch_shapes=[dma((times + 1,))],
        compiler_params=pltpu.CompilerParams(vmem_limit_bytes=8 << 20),
    )(grad, density)


def solution(mesh):
    return jax.shard_map(
        functools.partial(on_device, mesh.shape["tm"], mesh.shape["blk"]),
        mesh=mesh,
        in_specs=(
            P("tm", "blk", None, None, None),
            P(),
            P("blk", None),
            P("blk", None, None),
            P("blk", None, None),
            P("tm", None, None),
        ),
        out_specs=(P("tm", "blk", None, None), P("blk", None)),
        check_vma=False,
    )
```

```python
import functools
import math

import jax
import jax.numpy as jnp
from jax import lax
from jax.experimental import pallas as pl
from jax.experimental.pallas import tpu as pltpu
from jax.sharding import PartitionSpec as P

F32 = jnp.float32
BF16 = jnp.bfloat16
MESH = pl.DeviceIdType.MESH


def dot(a, b, dims=((1,), (0,)), precision=None):
    return lax.dot_general(a, b, (dims, ((), ())), preferred_element_type=F32, precision=precision)


def steps(count, body):
    if count <= 8:
        for i in range(count):
            body(i)
    else:
        lax.fori_loop(0, count, lambda i, c: (body(i), c)[1], 0)


def flip(index, offset, count):
    bit = 1
    while bit < count:
        if offset & bit:
            index = index + bit - 2 * bit * (index // bit % 2)
        bit *= 2
    return index


def kernel(
    n_tm, n_blk, parts, chunk,
    cos_hbm, partner_hbm, chi_ref, tens_ref, dens_ref, decay_ref,
    grad_ref, density_ref,
    cos_ref, partner_ref, partner_vec, chi_all, tens, dens, decay, sd, metric, corr,
    own_term, out_term, in_term, pair_vec, outgoing, arrived, coll,
    dpart_out, dpart_in,
    load_sem, chi_send, chi_recv, sib_send, sib_recv, vec_send, vec_recv,
    a2a_send, a2a_recv, dp_send, dp_recv,
):
    tm = lax.axis_index("tm")
    blk = lax.axis_index("blk")
    chips = n_blk // 2
    chip = blk // 2
    core = blk % 2
    n_pair, block, _ = chi_ref.shape
    times = decay.shape[0]
    half = times // 2
    rows2, width2 = tens.shape
    inv_width = 1.0 / math.sqrt(2 * width2)
    part = block // parts
    paired = n_tm & (n_tm - 1) == 0

    def tm_to(o):
        return flip(tm, o, n_tm) if paired else lax.rem(tm + o, n_tm)

    def tm_from(o):
        return flip(tm, o, n_tm) if paired else lax.rem(tm + n_tm - o, n_tm)

    tm_order = sorted(range(1, n_tm), key=lambda o: -bin(o).count("1"))

    barrier = pltpu.get_barrier_semaphore()
    for o in tm_order:
        pl.semaphore_signal(barrier, inc=1, device_id={"tm": tm_to(o)}, device_id_type=MESH)
    steps(n_blk - 1, lambda i: pl.semaphore_signal(
        barrier, inc=1, device_id={"blk": lax.rem(blk + i + 1, n_blk)}, device_id_type=MESH))

    loads = [
        pltpu.make_async_copy(chi_ref, chi_all.at[tm], load_sem.at[0]),
        pltpu.make_async_copy(partner_hbm, partner_ref, load_sem.at[1]),
        pltpu.make_async_copy(cos_hbm, cos_ref, load_sem.at[2]),
        pltpu.make_async_copy(decay_ref, decay, load_sem.at[3]),
        pltpu.make_async_copy(dens_ref.reshape(*dens.shape), dens, load_sem.at[4]),
        pltpu.make_async_copy(tens_ref.reshape(*tens.shape), tens, load_sem.at[5]),
    ]
    for copy in loads:
        copy.start()
    loads[0].wait()
    pl.semaphore_wait(barrier, n_tm + n_blk - 2)

    def chi_copy(o, r, source):
        rows = pl.ds(r * part, part)
        return pltpu.make_async_remote_copy(
            src_ref=chi_all.at[tm].at[:, rows, :],
            dst_ref=chi_all.at[source, :, rows, :],
            send_sem=chi_send.at[o - 1, r],
            recv_sem=chi_recv.at[o - 1, r],
            device_id={"tm": tm_to(o)},
            device_id_type=MESH,
        )

    for r in range(parts):
        for o in tm_order:
            chi_copy(o, r, tm).start()

    sibling = {"blk": chip * 2 + 1 - core}
    for copy in loads[1:3]:
        copy.wait()
    partner_vec[...] = jnp.full(partner_vec.shape, -1, jnp.int32)
    for k in range(n_pair):
        partner_vec[k : k + 1, :] = jnp.full((1, block), partner_ref[0, k], jnp.int32)
    vec_copy = pltpu.make_async_remote_copy(
        src_ref=partner_vec, dst_ref=pair_vec, send_sem=vec_send, recv_sem=vec_recv,
        device_id=sibling, device_id_type=MESH)
    vec_copy.start()

    for copy in loads[3:]:
        copy.wait()
    even = lax.broadcasted_iota(jnp.int32, (rows2, chunk), 0) % 2 == 0
    same = (lax.broadcasted_iota(jnp.int32, (rows2, rows2), 0) % 2) == (
        lax.broadcasted_iota(jnp.int32, (rows2, rows2), 1) % 2)
    spread = (
        lax.broadcasted_iota(jnp.int32, (rows2, block), 0) // 2
        == lax.broadcasted_iota(jnp.int32, (rows2, block), 1)
    ).astype(BF16)

    def halves(m):
        top = m.astype(BF16)
        return top, (m - top.astype(F32)).astype(BF16)

    def fold(m):
        a, b = halves(jnp.where(same, m, 0.0))
        m = dot(spread, a, ((0,), (0,))) + dot(spread, b, ((0,), (0,)))
        a, b = halves(m)
        return dot(a, spread) + dot(b, spread)

    for t in range(times):
        m2 = jnp.zeros((rows2, rows2), F32)
        for j in range(width2 // chunk):
            cols = slice(j * chunk, (j + 1) * chunk)
            factor = jnp.where(even, decay[t, 0:1, cols], decay[t, 1:2, cols])
            x = tens[:, cols]
            d = (dens[:, cols].astype(F32) * factor).astype(BF16)
            sd[t, :rows2, cols] = (x.astype(F32) * factor).astype(BF16)
            sd[t, rows2:, cols] = d
            m2 = m2 + dot(x, d, ((1,), (1,)))
        metric[t] = (fold(m2) * inv_width).astype(BF16)

    def sib_copy(r):
        return pltpu.make_async_remote_copy(
            src_ref=out_term.at[r], dst_ref=in_term.at[r],
            send_sem=sib_send.at[r], recv_sem=sib_recv.at[r],
            device_id=sibling, device_id_type=MESH)

    def other_chip(i):
        low = jnp.where(chips - 1 - i > chip, chips - 1 - i, chips - 2 - i)
        high = jnp.where(i < chip, i, i + 1)
        return jnp.where(chip < chips // 2, low, high)

    def a2a_copy(to_chip, to_core, r):
        dest = to_chip * 2 + to_core
        return pltpu.make_async_remote_copy(
            src_ref=outgoing.at[r, dest],
            dst_ref=arrived.at[chip, core, :, pl.ds(r * part, part), :],
            send_sem=a2a_send.at[to_chip, to_core, r],
            recv_sem=a2a_recv.at[chip, core, r],
            device_id={"blk": dest}, device_id_type=MESH)

    def a2a_arrival(from_chip, from_core, r):
        return pltpu.make_async_remote_copy(
            src_ref=outgoing.at[r, 0],
            dst_ref=arrived.at[from_chip, from_core, :, pl.ds(r * part, part), :],
            send_sem=a2a_send.at[from_chip, from_core, r],
            recv_sem=a2a_recv.at[from_chip, from_core, r],
            device_id=sibling, device_id_type=MESH)

    def terms(r):
        rows = pl.ds(r * part, part)
        for o in tm_order:
            chi_copy(o, r, tm_from(o)).wait_recv()
        for t in range(times):
            owner = (1 - core if t < half else core)
            slot = t % half
            time = owner * half + slot
            weights = [cos_ref[w, tm * times + time].astype(F32) / 1024.0 for w in range(n_tm)]
            m = metric[time]

            def some(first, count):
                g = weights[0] * chi_all[0, pl.ds(first, count), rows, :].astype(F32)
                for w in range(1, n_tm):
                    g = g + weights[w] * chi_all[w, pl.ds(first, count), rows, :].astype(F32)
                term = dot(g.astype(BF16).reshape(count * part, block), m).reshape(count, part, block)
                if t < half:
                    out_term[r, pl.ds(first, count), slot] = term.astype(BF16)
                else:
                    own_term[r, pl.ds(first, count), slot] = term

            if n_pair <= 8:
                some(0, n_pair)
            else:
                lax.fori_loop(0, n_pair, lambda k, c: (some(k, 1), c)[1], 0)
            if t == half - 1:
                sib_copy(r).start()

    def bins(r):
        sib_copy(r).wait_recv()

        def bin_of(dest):
            sums = []
            for slot in range(half):
                total = jnp.zeros((part, block), F32)

                def add(k, total):
                    mine = jnp.full((1, block), partner_ref[0, k], jnp.int32) == dest
                    theirs = pair_vec[pl.ds(k, 1), :] == dest
                    total = total + jnp.where(mine, own_term[r, k, slot], 0.0)
                    return total + jnp.where(theirs, in_term[r, k, slot].astype(F32), 0.0)

                if n_pair <= 8:
                    for k in range(n_pair):
                        total = add(k, total)
                else:
                    total = lax.fori_loop(0, n_pair, add, total)
                sums.append(total.astype(BF16))
            return sums

        def send(i):
            to_chip = other_chip(i)
            for c in range(2):
                for slot, total in enumerate(bin_of(to_chip * 2 + c)):
                    outgoing[r, to_chip * 2 + c, slot] = total
                a2a_copy(to_chip, c, r).start()

        steps(chips - 1, send)
        for slot, total in enumerate(bin_of(chip * 2 + 1 - core)):
            outgoing[r, chip * 2 + 1 - core, slot] = total
        a2a_copy(chip, 1 - core, r).start()
        for slot, total in enumerate(bin_of(blk)):
            arrived[chip, core, slot, r * part : (r + 1) * part] = total

    for r in range(parts + 1):
        if r < parts:
            terms(r)
        if r == 0:
            vec_copy.wait_recv()
        else:
            bins(r - 1)

    for t in range(times):
        for side in range(2):
            m2 = jnp.zeros((rows2, rows2), F32)
            for j in range(width2 // chunk):
                cols = slice(j * chunk, (j + 1) * chunk)
                m2 = m2 + dot(
                    sd[t, side * rows2 : (side + 1) * rows2, cols], sd[t, rows2:, cols], ((1,), (1,)))
            first = (2 * t + side) * block
            corr[first : first + block, :] = (fold(m2) * inv_width).astype(BF16)

    for r in range(parts):
        rows = slice(r * part, (r + 1) * part)
        a2a_arrival(chip, 1 - core, r).wait_recv()

        def wait_for(i):
            for c in range(2):
                a2a_arrival(other_chip(i), c, r).wait_recv()

        steps(chips - 1, wait_for)
        for t in range(times):

            def more(i, total):
                return total + arrived[i, t // half, t % half, rows].astype(F32)

            total = jnp.zeros((part, block), F32)
            if chips <= 8:
                for i in range(chips):
                    total = more(i, total)
            else:
                total = lax.fori_loop(0, chips, more, total)
            coll[rows, 2 * t * block : (2 * t + 1) * block] = total.astype(BF16)
    for t in range(times):
        turned = coll[:, 2 * t * block : (2 * t + 1) * block].astype(F32).T.astype(BF16)
        coll[:, (2 * t + 1) * block : (2 * t + 2) * block] = turned
    dpart_out[...] = dot(coll[...], corr[...]).astype(BF16)

    def dp_copy(o, source):
        return pltpu.make_async_remote_copy(
            src_ref=dpart_out, dst_ref=dpart_in.at[source],
            send_sem=dp_send.at[o - 1], recv_sem=dp_recv.at[o - 1],
            device_id={"tm": tm_to(o)}, device_id_type=MESH)

    for o in tm_order:
        dp_copy(o, tm).start()
    dpart_in[tm] = dpart_out[...]

    for t in range(times):
        wide = [
            jnp.where(same, dot(dot(spread, coll[:, i * block : (i + 1) * block]).astype(BF16), spread,
                                ((1,), (1,))), 0.0).astype(BF16)
            for i in (2 * t, 2 * t + 1)
        ]
        both = jnp.concatenate(wide, axis=1)
        for j in range(width2 // chunk):
            cols = slice(j * chunk, (j + 1) * chunk)
            grad_ref[t, :, cols] = dot(both, sd[t, :, cols]).astype(BF16)

    vec_copy.wait_send()
    for r in range(parts):
        for o in tm_order:
            chi_copy(o, r, tm).wait_send()
        sib_copy(r).wait_send()
        a2a_copy(chip, 1 - core, r).wait_send()

        def sent(i):
            for c in range(2):
                a2a_copy(other_chip(i), c, r).wait_send()

        steps(chips - 1, sent)
    for o in tm_order:
        dp_copy(o, tm_from(o)).wait_recv()
    density = dpart_in[0].astype(F32)
    for w in range(1, n_tm):
        density = density + dpart_in[w].astype(F32)
    density_ref[...] = density
    for o in tm_order:
        dp_copy(o, tm).wait_send()


def deliver(grad_ref, density_ref, grad_out, density_out, sem):
    copies = [
        pltpu.make_async_copy(grad_ref.at[t], grad_out.at[t].reshape(*grad_ref.shape[1:]), sem.at[t])
        for t in range(grad_ref.shape[0])
    ]
    copies.append(pltpu.make_async_copy(density_ref, density_out, sem.at[len(copies)]))
    for copy in copies:
        copy.start()
    for copy in copies:
        copy.wait()


def on_device(n_tm, n_blk, chi_bar, cos_table, partner, tensor, dens_tensor, decay):
    n_pair, block = chi_bar.shape[2], chi_bar.shape[3]
    times = decay.shape[0]
    half = times // 2
    rows2, width2 = block * tensor.shape[1], tensor.shape[2]
    chips = n_blk // 2
    parts = 4
    chunk = 512
    part = block // parts
    any_ = pl.BlockSpec(memory_space=pl.ANY)
    vmem = pl.BlockSpec(memory_space=pltpu.VMEM)
    pad = -n_pair % 8
    dma = pltpu.SemaphoreType.DMA
    grad, density = pl.pallas_call(
        functools.partial(kernel, n_tm, n_blk, parts, chunk),
        out_shape=(
            pltpu.VMEM((times, rows2, width2), BF16),
            pltpu.VMEM((block, block), F32),
        ),
        in_specs=[any_] * 6,
        out_specs=(vmem, vmem),
        scratch_shapes=[
            pltpu.SMEM(cos_table.shape[::-1], jnp.int32),
            pltpu.SMEM(partner.shape, jnp.int32),
            pltpu.VMEM((n_pair + pad, block), jnp.int32),
            pltpu.VMEM((n_tm, n_pair, block, block), BF16),
            pltpu.VMEM((rows2, width2), BF16),
            pltpu.VMEM((rows2, width2), BF16),
            pltpu.VMEM(decay.shape, F32),
            pltpu.VMEM((times, 2 * rows2, width2), BF16),
            pltpu.VMEM((times, block, block), BF16),
            pltpu.VMEM((times * 2 * block, block), BF16),
            pltpu.VMEM((parts, n_pair, half, part, block), F32),
            pltpu.VMEM((parts, n_pair, half, part, block), BF16),
            pltpu.VMEM((parts, n_pair, half, part, block), BF16),
            pltpu.VMEM((n_pair + pad, block), jnp.int32),
            pltpu.VMEM((parts, n_blk, half, part, block), BF16),
            pltpu.VMEM((chips, 2, half, block, block), BF16),
            pltpu.VMEM((block, times * 2 * block), BF16),
            pltpu.VMEM((block, block), BF16),
            pltpu.VMEM((n_tm, block, block), BF16),
            dma((6,)),
            dma((n_tm - 1, parts)), dma((n_tm - 1, parts)),
            dma((parts,)), dma((parts,)),
            dma, dma,
            dma((chips, 2, parts)), dma((chips, 2, parts)),
            dma((n_tm - 1,)), dma((n_tm - 1,)),
        ],
        compiler_params=pltpu.CompilerParams(collective_id=0, has_side_effects=True),
    )(
        cos_table.T, partner,
        chi_bar.reshape(n_pair, block, block),
        tensor, dens_tensor, decay,
    )
    return pl.pallas_call(
        deliver,
        out_shape=(
            jax.ShapeDtypeStruct((times, *tensor.shape), BF16),
            jax.ShapeDtypeStruct((block, block), F32),
        ),
        in_specs=[vmem, vmem],
        out_specs=(any_, any_),
        scratch_shapes=[dma((times + 1,))],
        compiler_params=pltpu.CompilerParams(vmem_limit_bytes=8 << 20),
    )(grad, density)


def solution(mesh):
    return jax.shard_map(
        functools.partial(on_device, mesh.shape["tm"], mesh.shape["blk"]),
        mesh=mesh,
        in_specs=(
            P("tm", "blk", None, None, None),
            P(),
            P("blk", None),
            P("blk", None, None),
            P("blk", None, None),
            P("tm", None, None),
        ),
        out_specs=(P("tm", "blk", None, None), P("blk", None)),
        check_vma=False,
    )
```
